32 devices in a mesh: ctx: 16 (over z, y, core), head: 2 (over x).
Axes of the slice: x: 2, y: 2, z: 4, core: 2. Of those that a mesh axis runs over, the one named last changes fastest.
Arguments:
- fine_query: bfloat16 [4096, 4096], P('ctx', 'head'), may hold values from -181 to 181
- fine_memory: bfloat16 [2, 4096, 1024], P(None, 'ctx', 'head'), may hold values from -6.5 to 6.5
- coarse_query: bfloat16 [2048, 4096], P('ctx', 'head'), may hold values from -181 to 181
- coarse_memory: bfloat16 [2, 2048, 1024], P(None, 'ctx', 'head'), may hold values from -6.5 to 6.5
- coarse_scale: int32 [2048], P('ctx'), may hold values from 0 to 7, never falling along the last dimension, each value on 1 to 512 neighbouring positions
- out_weight: bfloat16 [4096, 4096], P('head'), may hold values from -0.09375 to 0.09375
Outputs:
- fine_mixed: bfloat16 [4096, 4096], P(('ctx', 'head'))
- coarse_mixed: bfloat16 [2048, 4096], P(('ctx', 'head'))
The draws below stay inside these ranges and needn't reach their ends.
Inputs may be any that keep to these rules, and one draw needn't show every extreme that they name: `coarse_scale`: never falls along the coarse tokens.
All inputs are finite; a program needn't handle non-finite values.
Results may differ from the reference program's by a relative error of at most 0.014.
Values may be sent and summed in bfloat16 or wider, within the bound.
A program may use at most 128 MiB of HBM per device.

```python
import math
import jax
import jax.numpy as jnp
import numpy as np
from jax import lax

D = 4096
QH = 32
KVH = 8
HD = 128
SCALES = 8
FINE = 4096
COARSE = 2048


def drawn_keys(key, length, width, salt):
    base = jax.random.truncated_normal(jax.random.fold_in(key, salt), -6.0, 6.0, (length, width), jnp.float32)
    return base


def drawn_queries(key, length, salt_query):
    query = 2.5 * jax.random.truncated_normal(jax.random.fold_in(key, salt_query), -6.0, 6.0, (length, QH * HD), jnp.float32)
    return query


def memory_pair(key, length, salt_keys, salt_values):
    keyset = drawn_keys(key, length, KVH * HD, salt_keys)
    valueset = jax.random.truncated_normal(jax.random.fold_in(key, salt_values), -6.0, 6.0, (length, KVH * HD), jnp.float32)
    return jnp.stack([keyset, valueset]).astype(jnp.bfloat16)


def draw_fine_query(key, part):
    return drawn_queries(key, FINE, 17).astype(jnp.bfloat16)


def draw_fine_memory(key, part):
    return memory_pair(key, FINE, 11, 13)


def draw_coarse_query(key, part):
    return drawn_queries(key, COARSE, 27).astype(jnp.bfloat16)


def draw_coarse_memory(key, part):
    return memory_pair(key, COARSE, 21, 23)


def steps_of(key, extent, split, smallest, largest):
    loudness = 1.0
    for axis_at, blocks in split:
        steps = jax.random.uniform(jax.random.fold_in(jax.random.fold_in(key, 6), axis_at), (blocks,), jnp.float32, smallest / len(split), largest / len(split))
        loudness = loudness * jnp.repeat(jnp.exp(steps), extent[axis_at] // blocks).reshape((-1,) + (1,) * (len(extent) - 1 - axis_at))
    return loudness


def length_profile(count, total, most, lean):
    weights = [(1 << 20) // math.isqrt(rank ** lean) + 1 for rank in range(2, count + 1)]
    surplus, given = total - most - (count - 1), [1] * (count - 1)
    while surplus > 0:
        candidates = [i for i in range(count - 1) if given[i] < most]
        mass, left = sum([weights[i] for i in candidates]), surplus
        for i in candidates:
            extra = min(most - given[i], max(1, left * weights[i] // mass), surplus)
            given[i] = given[i] + extra
            surplus = surplus - extra
    return np.array([most] + given)


def ragged(rng, amount, total, limit, slope):
    if amount == 2:
        one = jax.random.randint(rng, (), max(1, total - limit), min(limit, total - 1) + 1)
        return jnp.stack([one, total - one])
    tallies = jnp.asarray(length_profile(amount, total, limit, slope), jnp.int32)
    couples = (amount - 1) // 2
    source_of, receiver = tallies[1:1 + 2 * couples:2], tallies[2:2 + 2 * couples:2]
    slack = jnp.minimum(source_of - 1, limit - receiver)
    moved = jax.random.randint(jax.random.fold_in(rng, 1), (couples,), 0, 1 << 20) % (slack + 1)
    tallies = tallies.at[1:1 + 2 * couples:2].set(source_of - moved).at[2:2 + 2 * couples:2].set(receiver + moved)
    return tallies[jax.random.permutation(jax.random.fold_in(rng, 2), amount)]


def centred(rng, dims, scale, limit, split=(), dtype=jnp.bfloat16):
    values = jax.random.normal(rng, dims, jnp.float32) * scale
    if len(split) > 0:
        values = steps_of(rng, dims, split, -0.22, 0.18) * values
    return jnp.clip(values, min=-limit, max=limit).astype(dtype)


def setup_inputs(seed: int = 0) -> dict:
    key_of = jax.random.split(jax.random.key(seed), 7)
    fine_query = draw_fine_query(jax.random.fold_in(key_of[6], 71), 0)
    fine_memory = draw_fine_memory(jax.random.fold_in(key_of[6], 71), 0)
    coarse_query = draw_coarse_query(jax.random.fold_in(key_of[6], 71), 0)
    coarse_memory = draw_coarse_memory(jax.random.fold_in(key_of[6], 71), 0)
    coarse_scale = jnp.searchsorted(jnp.cumsum(ragged(key_of[4], SCALES, COARSE, COARSE // 4, 1)), jnp.arange(COARSE), side="right").astype(jnp.int32)
    out_weight = centred(key_of[5], (QH * HD, D), (QH * HD) ** -0.5, 0.09375, ((0, 2),))
    return {"fine_query": fine_query, "fine_memory": fine_memory, "coarse_query": coarse_query, "coarse_memory": coarse_memory, "coarse_scale": coarse_scale, "out_weight": out_weight}


masked_score = -1e30


def attend(queries, key_rows, value_rows, q_level, k_level):
    length = queries.shape[0]
    grouped = queries.astype(jnp.float32).reshape(length, KVH, QH // KVH, HD)
    key_heads = key_rows.astype(jnp.float32).reshape(-1, KVH, HD)
    value_heads = value_rows.astype(jnp.float32).reshape(-1, KVH, HD)
    scores = jnp.einsum('rkgd,skd->kgrs', grouped, key_heads) * (HD ** -0.5)
    allowed = k_level[None, :] <= q_level[:, None]
    scores = jnp.where(allowed[None, None], scores, masked_score)
    highest = jnp.max(scores, axis=-1, keepdims=True)
    shifted = jnp.exp(scores - highest)
    totals = jnp.sum(shifted, axis=-1)
    weights = lax.optimization_barrier(shifted.astype(jnp.bfloat16)).astype(jnp.float32)
    result = jnp.einsum('kgrs,skd->kgrd', weights, value_heads) / totals[..., None]
    return result.transpose(2, 0, 1, 3).reshape(length, QH * HD).astype(jnp.bfloat16)


def run_rows(queries, q_level, key_rows, value_rows, k_level):
    width = queries.shape[1]
    query_blocks = queries.reshape(-1, 64, width)
    level_blocks = q_level.reshape(-1, 64)
    mapped = lax.map(lambda pair: attend(pair[0], key_rows, value_rows, pair[1], k_level), (query_blocks, level_blocks))
    return mapped.reshape(-1, width)


def reference(fine_query, fine_memory, coarse_query, coarse_memory, coarse_scale, out_weight):
    fine_level = jnp.full((FINE,), SCALES, jnp.int32)
    all_keys = jnp.concatenate([fine_memory[0], coarse_memory[0]], axis=0)
    all_values = jnp.concatenate([fine_memory[1], coarse_memory[1]], axis=0)
    all_levels = jnp.concatenate([fine_level, coarse_scale.astype(jnp.int32)], axis=0)
    fine_attention = run_rows(fine_query, fine_level, all_keys, all_values, all_levels)
    coarse_attention = run_rows(coarse_query, coarse_scale.astype(jnp.int32), coarse_memory[0], coarse_memory[1], coarse_scale.astype(jnp.int32))
    fine_mixed = jnp.dot(fine_attention, out_weight, preferred_element_type=jnp.float32).astype(jnp.bfloat16)
    coarse_mixed = jnp.dot(coarse_attention, out_weight, preferred_element_type=jnp.float32).astype(jnp.bfloat16)
    return fine_mixed, coarse_mixed
```

```python
import functools
import math

import jax
import jax.numpy as jnp
from jax import lax
from jax.experimental import pallas as pl
from jax.experimental.pallas import tpu as pltpu
from jax.sharding import PartitionSpec as P

HD = 128
MASKED = -1e30
LOG2E = math.log2(math.e)


def split_queries(rows):
    scaled = rows.astype(jnp.float32) * (HD ** (-0.5) * LOG2E)
    high = scaled.astype(jnp.bfloat16)
    low = (scaled - high.astype(jnp.float32)).astype(jnp.bfloat16)
    return jnp.concatenate([high, low], axis=1)


def scores_of(keys, pair):
    doubled = jnp.concatenate([keys, keys], axis=1)
    return lax.dot_general(
        doubled, pair, (((1,), (1,)), ((), ())), preferred_element_type=jnp.float32
    )


def fold(state, scores, values_t):
    highest, total, weighted = state
    new = jnp.maximum(highest, jnp.max(scores, axis=0, keepdims=True))
    rescale = jnp.exp2(highest - new)
    shifted = jnp.exp2(scores - new)
    total = total * rescale + jnp.sum(shifted, axis=0, keepdims=True)
    weighted = weighted * rescale + jnp.dot(
        values_t, shifted.astype(jnp.bfloat16), preferred_element_type=jnp.float32
    )
    return (new, total, weighted)


def start(columns):
    return (
        jnp.full((1, columns), MASKED, jnp.float32),
        jnp.zeros((1, columns), jnp.float32),
        jnp.zeros((HD, columns), jnp.float32),
    )


def attention_kernel(
    ratio, span, fq_ref, fkv_ref, cq_ref, ckv_ref, qlev_ref, klev_ref, fo_ref, co_ref, vt_ref
):
    fine_keys, coarse_keys = fkv_ref.shape[1], ckv_ref.shape[1]
    rows, coarse_rows = fq_ref.shape[0], cq_ref.shape[0]
    chunks = [(ckv_ref, at, at) for at in range(0, coarse_keys, span)]
    coarse_count = len(chunks)
    chunks += [(fkv_ref, at, coarse_keys + at) for at in range(0, fine_keys, span)]
    for ref, at, to in chunks:
        vt_ref[:, to : to + span] = ref[1, at : at + span, :].T

    def run(pair, count, allowed):
        state = start(pair.shape[0])

        def scored(which):
            ref, at, to = chunks[which]
            scores = scores_of(ref[0, at : at + span, :], pair)
            return allowed(scores, at)

        ahead = scored(0)
        for which in range(count):
            scores = ahead
            if which + 1 < count:
                ahead = scored(which + 1)
            to = chunks[which][2]
            state = fold(state, scores, vt_ref[:, to : to + span])
        return (state[2] / state[1]).T.astype(jnp.bfloat16)

    @pl.loop(0, ratio)
    def _(head):
        columns = pl.ds(pl.multiple_of(head * HD, HD), HD)
        fo_ref[:, columns] = run(
            split_queries(fq_ref[:, columns]), len(chunks), lambda scores, at: scores
        )

    stack = 2 if ratio % 2 == 0 else 1
    levels = jnp.concatenate([qlev_ref[...]] * stack, axis=1)

    def masked(scores, at):
        return jnp.where(klev_ref[at : at + span, :] <= levels, scores, MASKED)

    @pl.loop(0, ratio // stack)
    def _(part):
        heads = [
            pl.ds(pl.multiple_of((part * stack + i) * HD, HD), HD) for i in range(stack)
        ]
        pair = jnp.concatenate([split_queries(cq_ref[:, columns]) for columns in heads], axis=0)
        result = run(pair, coarse_count, masked)
        for i, columns in enumerate(heads):
            co_ref[:, columns] = result[i * coarse_rows : (i + 1) * coarse_rows]


def attention(fine_query, fine_kv, coarse_query, coarse_kv, query_levels, key_levels):
    groups = fine_kv.shape[2] // HD
    width = fine_query.shape[1] // groups
    ratio = width // HD
    rows, coarse_rows = fine_query.shape[0], coarse_query.shape[0]
    fine_keys, coarse_keys = fine_kv.shape[1], coarse_kv.shape[1]
    span = math.gcd(math.gcd(fine_keys, coarse_keys), 512)
    return pl.pallas_call(
        functools.partial(attention_kernel, ratio, span),
        grid=(groups,),
        out_shape=(
            jax.ShapeDtypeStruct(fine_query.shape, jnp.bfloat16),
            jax.ShapeDtypeStruct(coarse_query.shape, jnp.bfloat16),
        ),
        in_specs=[
            pl.BlockSpec((rows, width), lambda g: (0, g)),
            pl.BlockSpec((2, fine_keys, HD), lambda g: (0, 0, g)),
            pl.BlockSpec((coarse_rows, width), lambda g: (0, g)),
            pl.BlockSpec((2, coarse_keys, HD), lambda g: (0, 0, g)),
            pl.BlockSpec((1, coarse_rows), lambda g: (0, 0)),
            pl.BlockSpec((coarse_keys, 1), lambda g: (0, 0)),
        ],
        out_specs=(
            pl.BlockSpec((rows, width), lambda g: (0, g)),
            pl.BlockSpec((coarse_rows, width), lambda g: (0, g)),
        ),
        scratch_shapes=[pltpu.VMEM((HD, fine_keys + coarse_keys), jnp.bfloat16)],
        compiler_params=pltpu.CompilerParams(vmem_limit_bytes=50 << 20),
    )(fine_query, fine_kv, coarse_query, coarse_kv, query_levels, key_levels)


def per_device(fine_query, fine_memory, coarse_query, coarse_memory, coarse_scale, out_weight):
    levels = coarse_scale.astype(jnp.float32)
    key_levels = lax.all_gather(
        levels.astype(jnp.bfloat16).reshape(1, -1), "ctx", axis=1, tiled=True
    )
    coarse_kv = lax.all_gather(coarse_memory, "ctx", axis=1, tiled=True)
    fine_kv = lax.all_gather(fine_memory, "ctx", axis=1, tiled=True)
    fine_attention, coarse_attention = attention(
        fine_query,
        fine_kv,
        coarse_query,
        coarse_kv,
        levels.reshape(1, -1),
        key_levels.astype(jnp.float32).reshape(-1, 1),
    )

    def mix(rows):
        partial = jnp.dot(rows, out_weight, preferred_element_type=jnp.float32)
        return lax.psum_scatter(
            partial.astype(jnp.bfloat16), "head", scatter_dimension=0, tiled=True
        )

    return (mix(fine_attention), mix(coarse_attention))


def solution(mesh):
    placed = (
        P("ctx", "head"),
        P(None, "ctx", "head"),
        P("ctx", "head"),
        P(None, "ctx", "head"),
        P("ctx"),
        P("head", None),
    )
    return jax.shard_map(
        per_device,
        mesh=mesh,
        in_specs=placed,
        out_specs=(P(("ctx", "head"), None), P(("ctx", "head"), None)),
        check_vma=False,
    )
```
